128 devices in a mesh: row: 8 (over z_lo, y), col: 16 (over x, z_hi, core).
Axes of the slice: x: 4, y: 4, z: 4 (z_hi: 2, z_lo: 2; z = z_hi * 2 + z_lo), core: 2. Of those that a mesh axis runs over, the one named last changes fastest.
Arguments:
- density: bfloat16 [16, 64, 32768], P('row', None, 'col'), may hold values from -0.8984375 to 0.8984375
- density_rows: int32 [16, 16, 32], replicated, may hold values from 0 to 48, as said below
- square_rows: int32 [16, 16, 32], replicated, may hold values from 0 to 48, as said below
- panel_shift: int32 [16], replicated, may hold values from 0 to 48
Outputs:
- purified: float32 [16, 64, 32768], P('row', None, 'col')
The draws below stay inside these ranges and needn't reach their ends.
Inputs may be any that keep to these rules, and one draw needn't show every extreme that they name: `density_rows`: for every tile, 32 distinct block rows in increasing order. `square_rows`: for every tile, 32 distinct block rows in increasing order.
All inputs are finite; a program needn't handle non-finite values.
Results may differ from the reference program's by a relative error of at most 0.0029.
Values may be sent and summed in bfloat16 or wider, within the bound.
A program may use at most 64 MiB of HBM per device.

```python
import jax
import jax.numpy as jnp
from jax import lax

BLOCK = 64
PANEL = 49
RH = 32
NPAN = 16
N_COL = 16


def draw_rows_common(key):
    scores = jax.random.randint(key, (N_COL, N_COL, PANEL), 0, 1048576) * PANEL
    scores = scores + jnp.arange(PANEL, dtype=jnp.int32)[None, None, :]
    order = jnp.argsort(scores, axis=-1, stable=True).astype(jnp.int32)
    return jnp.sort(order[:, :, :RH], axis=-1).astype(jnp.int32)


def draw_density_rows(key, part):
    return draw_rows_common(jax.random.fold_in(key, 11))


def draw_square_rows(key, part):
    return draw_rows_common(jax.random.fold_in(key, 23))


def set_ends(drawn, stream_key, least, largest):
    dims = drawn.shape
    place = [jax.random.randint(jax.random.fold_in(stream_key, axis), (), 0, dims[axis]) for axis in range(len(dims))]
    drawn = drawn.at[tuple(place)].set(least)
    longest = dims.index(max(dims))
    place[longest] = (place[longest] + 1) % dims[longest]
    return drawn.at[tuple(place)].set(largest)


def block_levels(key, dims, split, low, largest):
    gain = 1.0
    for axis_at, parts in split:
        heights = jax.random.uniform(jax.random.fold_in(jax.random.fold_in(key, 6), axis_at), (parts,), jnp.float32, low / len(split), largest / len(split))
        gain = gain * jnp.repeat(jnp.exp(heights), dims[axis_at] // parts).reshape((-1,) + (1,) * (len(dims) - 1 - axis_at))
    return gain


def noise(own_key, extent, deviation, limit, shards=(), kind=jnp.bfloat16):
    entries = deviation * jax.random.normal(own_key, extent, jnp.float32)
    if shards:
        entries = entries * block_levels(own_key, extent, shards, -0.22, 0.18)
    return jnp.clip(entries, -limit, limit).astype(kind)


def setup_inputs(seed: int = 0) -> dict:
    arg_keys = jax.random.split(jax.random.key(seed), 5)
    density = noise(arg_keys[0], (NPAN, BLOCK, NPAN * RH * BLOCK), 0.15, 0.8984375, ((0, 8), (2, 16)))
    density_rows = draw_density_rows(jax.random.fold_in(arg_keys[4], 71), 0)
    square_rows = draw_square_rows(jax.random.fold_in(arg_keys[4], 71), 0)
    panel_shift = set_ends(jax.random.randint(arg_keys[3], (NPAN,), 0, PANEL), jax.random.fold_in(arg_keys[3], 1), 0, PANEL - 1).astype(jnp.int32)
    return dict(density=density, density_rows=density_rows, square_rows=square_rows, panel_shift=panel_shift)


def tile_product(left_vals, left_rows, right_vals, right_rows, out_rows, panel_shift):
    npan = left_rows.shape[0]
    blk = left_vals.shape[1]
    rh = left_rows.shape[2]
    left_t = jnp.transpose(left_vals.reshape(npan, blk, npan, rh, blk), (0, 2, 3, 1, 4))
    right_t = jnp.transpose(right_vals.reshape(npan, blk, npan, rh, blk), (0, 2, 3, 1, 4))
    slots = jnp.arange(rh, dtype=jnp.int32)
    panels = jnp.arange(npan, dtype=jnp.int32)
    right_rows_t = jnp.transpose(right_rows, (1, 0, 2))

    def one_panel(p):
        crow = out_rows[p]
        arow = left_rows[p]
        match_a = arow[None, None, :, :] == crow[:, :, None, None]
        has_a = jnp.any(match_a, axis=-1)
        a_index = jnp.sum(jnp.where(match_a, slots, 0), axis=-1).astype(jnp.int32)
        target = jnp.mod(crow[:, :, None] + panel_shift[None, None, :] - panel_shift[p], PANEL).astype(jnp.int32)
        match_b = right_rows_t[:, None, :, :] == target[:, :, :, None]
        has_b = jnp.any(match_b, axis=-1)
        b_index = jnp.sum(jnp.where(match_b, slots, 0), axis=-1).astype(jnp.int32)
        a_blocks = left_t[p][panels[None, None, :], a_index].astype(jnp.float32)
        b_blocks = right_t[panels[None, None, :], panels[:, None, None], b_index].astype(jnp.float32)
        weight = jnp.logical_and(has_a, has_b).astype(jnp.float32)
        a_blocks = a_blocks * weight[:, :, :, None, None]
        return jnp.einsum('qekxy,qekyz->qexz', a_blocks, b_blocks)

    result = lax.map(one_panel, panels)
    return jnp.transpose(result, (0, 3, 1, 2, 4)).reshape(npan, blk, npan * rh * blk)


def reference(density, density_rows, square_rows, panel_shift):
    square = tile_product(density, density_rows, density, density_rows, square_rows, panel_shift).astype(jnp.bfloat16)
    cube = tile_product(square, square_rows, density, density_rows, square_rows, panel_shift)
    return 3.0 * square.astype(jnp.float32) - 2.0 * cube
```

```python
import jax
import jax.numpy as jnp
from jax import lax
from jax.experimental import pallas as pl
from jax.experimental.pallas import tpu as pltpu
from jax.sharding import PartitionSpec as P

PANEL = 49
BLOCK = 64
SPAN = 2 * BLOCK
RH = 32
NPAN = 16
N_ROW = 8
N_COL = 16
HALF = NPAN * BLOCK // 2
FULL = NPAN * BLOCK
MESH = pl.DeviceIdType.MESH


def home(u):
    last = u // (PANEL - 1)
    x = (u // 12) % 4
    y = (u // 3) % 4
    d = (u % 3 + 1) * (1 - last)
    z = (d + 8 - x - y) % 4
    return (z % 2) * 4 + y, x * 4 + (z // 2) * 2


def low_high(a, b):
    low = jnp.concatenate([a[:, :BLOCK], b[:, :BLOCK]], axis=1)
    high = jnp.concatenate([a[:, BLOCK:], b[:, BLOCK:]], axis=1)
    return low, high


def kernel(
    src_ref, shift_ref, x_ref, srows_ref, out_ref,
    pairs, send, recv, mat, acc, sq, mask, back,
    send_sem, recv_sem, sib_send, sib_recv, back_send, back_recv,
):
    row = lax.axis_index("row")
    col = lax.axis_index("col")
    core = col % 2
    y = row % 4
    z_lo = row // 4
    x = col // 4
    z = 2 * ((col // 2) % 2) + z_lo
    d = (x + y + z) % 4
    corner = (row + col // 2) == 0
    works = jnp.logical_or(d != 0, corner)
    mine = jnp.where(corner, PANEL - 1, (x * 4 + y) * 3 + d - 1)
    own = jnp.logical_and(works, core == z_lo)
    n_own = own.astype(jnp.int32)
    sibling = col + 1 - 2 * core

    barrier = pltpu.get_barrier_semaphore()
    pl.semaphore_signal(barrier, inc=1, device_id=(row, sibling), device_id_type=MESH)

    @pl.when(works)
    def _():
        def greet(s, carry):
            to_row, to_col = 4 * core + s // N_COL, s % N_COL

            @pl.when(jnp.logical_or(to_row != row, to_col != col))
            def _():
                pl.semaphore_signal(barrier, inc=1, device_id=(to_row, to_col), device_id_type=MESH)

            return carry

        lax.fori_loop(0, 4 * N_COL, greet, 0)

    pl.semaphore_wait(barrier, PANEL + 1 - n_own)

    lane = lax.broadcasted_iota(jnp.int32, (1, SPAN), 1)
    left = jnp.where(lane < BLOCK, 1.0, 0.0)
    right = 1.0 - left

    start = (row * N_COL + col) * PANEL // (N_ROW * N_COL)

    for tile in range(2):
        for m in range(RH // 2):
            pairs[tile * (RH // 2) + m] = x_ref[tile, :, m * SPAN : (m + 1) * SPAN]

    def fetch(t, carry):
        u = (start + t) % PANEL
        parts = []
        for tile, side in ((0, left), (1, right)):
            entry = src_ref[tile * PANEL + u]
            has = (entry // RH).astype(jnp.float32)
            e = entry % RH
            wide = pairs[tile * (RH // 2) + e // 2]
            turned = jnp.concatenate([wide[:, BLOCK:], wide[:, :BLOCK]], axis=1)
            picked = jnp.where(e % 2 == tile, wide, turned)
            parts.append(picked * (side * has).astype(jnp.bfloat16))
        send[u] = parts[0] + parts[1]
        to_row, to_first = home(u)
        to_col = to_first + z_lo
        is_self = jnp.logical_and(to_row == row, to_col == col)

        @pl.when(jnp.logical_not(is_self))
        def _():
            pltpu.make_async_remote_copy(
                src_ref=send.at[u],
                dst_ref=recv.at[y, col],
                send_sem=send_sem,
                recv_sem=recv_sem.at[y],
                device_id=(to_row, to_col),
                device_id_type=MESH,
            ).start()

        @pl.when(is_self)
        def _():
            pltpu.make_async_copy(send.at[u], recv.at[y, col], recv_sem.at[y]).start()

        return carry

    lax.fori_loop(0, PANEL, fetch, 0)

    @pl.when(works)
    def _():
        half = pl.multiple_of(core * HALF, HALF)
        there = pl.multiple_of((1 - core) * HALF, HALF)

        spread = jnp.where(
            lax.broadcasted_iota(jnp.int32, (NPAN, FULL), 1) // BLOCK
            == lax.broadcasted_iota(jnp.int32, (NPAN, FULL), 0),
            1.0,
            0.0,
        ).astype(jnp.bfloat16)
        for k in range(NPAN // 2):
            p = core * (NPAN // 2) + k
            past = srows_ref[p] - shift_ref[p]
            hit = jnp.logical_or(past == mine, past == mine - PANEL)
            hit = jnp.where(hit, 1.0, 0.0).astype(jnp.bfloat16)
            count = lax.dot_general(
                jnp.ones((8, RH), jnp.bfloat16), hit, (((1,), (1,)), ((), ())),
                preferred_element_type=jnp.float32,
            ).astype(jnp.bfloat16)
            mask[k] = jnp.dot(count, spread, preferred_element_type=jnp.float32)

        def arrive(g, carry):
            pltpu.make_async_copy(recv.at[g], recv.at[g], recv_sem.at[g]).wait()
            base = pl.multiple_of(core * HALF + g * SPAN, SPAN)
            for c in range(N_COL // 2):
                low, high = low_high(recv[g, 2 * c], recv[g, 2 * c + 1])
                mat[pl.ds(base, BLOCK), pl.ds(c * SPAN, SPAN)] = low
                mat[pl.ds(base + BLOCK, BLOCK), pl.ds(c * SPAN, SPAN)] = high
            pltpu.make_async_remote_copy(
                src_ref=mat.at[pl.ds(base, SPAN)],
                dst_ref=mat.at[pl.ds(base, SPAN)],
                send_sem=sib_send.at[g],
                recv_sem=sib_recv.at[g],
                device_id=(row, sibling),
                device_id_type=MESH,
            ).start()
            return carry

        lax.fori_loop(0, 4, arrive, 0)

        def first(n, carry):
            at = pl.multiple_of(n * 256, 256)
            acc[:, pl.ds(at, 256)] = jnp.dot(
                mat[pl.ds(half, HALF), pl.ds(half, HALF)],
                mat[pl.ds(half, HALF), pl.ds(at, 256)],
                preferred_element_type=jnp.float32,
            )
            return carry

        lax.fori_loop(0, FULL // 256, first, 0)

        def met(g, carry):
            sent = pl.multiple_of(half + g * SPAN, SPAN)
            came = pl.multiple_of(there + g * SPAN, SPAN)
            copy = pltpu.make_async_remote_copy(
                src_ref=mat.at[pl.ds(sent, SPAN)],
                dst_ref=mat.at[pl.ds(came, SPAN)],
                send_sem=sib_send.at[g],
                recv_sem=sib_recv.at[g],
                device_id=(row, sibling),
                device_id_type=MESH,
            )
            copy.wait_send()
            copy.wait_recv()
            return carry

        lax.fori_loop(0, 4, met, 0)

        def second(n, carry):
            at = pl.multiple_of(n * 256, 256)
            more = jnp.dot(
                mat[pl.ds(half, HALF), pl.ds(there, HALF)],
                mat[pl.ds(there, HALF), pl.ds(at, 256)],
                preferred_element_type=jnp.float32,
            )
            whole = acc[:, pl.ds(at, 256)] + more
            for k in range(NPAN // 2):
                keep = mask[k, 0:1, pl.ds(at, 256)]
                sq[k * BLOCK : (k + 1) * BLOCK, pl.ds(at, 256)] = (
                    whole[k * BLOCK : (k + 1) * BLOCK] * keep
                ).astype(jnp.bfloat16)
            return carry

        lax.fori_loop(0, FULL // 256, second, 0)

        def third(n, carry):
            at = pl.multiple_of(n * 256, 256)
            cube = jnp.dot(sq[...], mat[:, pl.ds(at, 256)], preferred_element_type=jnp.float32)
            done = (3.0 * sq[:, pl.ds(at, 256)].astype(jnp.float32) - 2.0 * cube).astype(jnp.bfloat16)
            for g in range(4):
                for c in range(2):
                    top = done[g * SPAN : g * SPAN + BLOCK, c * SPAN : (c + 1) * SPAN]
                    low_part = done[g * SPAN + BLOCK : (g + 1) * SPAN, c * SPAN : (c + 1) * SPAN]
                    low, high = low_high(top, low_part)
                    back[g, 4 * n + 2 * c] = low
                    back[g, 4 * n + 2 * c + 1] = high

            def post(i, inner):
                g, j = i // 4, 4 * n + i % 4
                to_row = 4 * core + g
                is_self = jnp.logical_and(to_row == row, j == col)

                @pl.when(jnp.logical_not(is_self))
                def _():
                    pltpu.make_async_remote_copy(
                        src_ref=back.at[g, j],
                        dst_ref=out_ref.at[mine],
                        send_sem=back_send,
                        recv_sem=back_recv,
                        device_id=(to_row, j),
                        device_id_type=MESH,
                    ).start()

                @pl.when(is_self)
                def _():
                    pltpu.make_async_copy(back.at[g, j], out_ref.at[mine], back_recv).start()

                return inner

            lax.fori_loop(0, 16, post, 0)
            return carry

        lax.fori_loop(0, FULL // 256, third, 0)

    @pl.when(own)
    def _():
        most = send.at[pl.ds(0, PANEL - 1)]
        pltpu.make_async_copy(most, most, send_sem).wait()

    @pl.when(jnp.logical_not(own))
    def _():
        pltpu.make_async_copy(send, send, send_sem).wait()

    @pl.when(own)
    def _():
        flat = back.reshape(4 * N_COL, BLOCK, SPAN).at[pl.ds(0, 4 * N_COL - 1)]
        pltpu.make_async_copy(flat, flat, back_send).wait()

    @pl.when(jnp.logical_and(works, jnp.logical_not(own)))
    def _():
        pltpu.make_async_copy(back, back, back_send).wait()

    pltpu.make_async_copy(out_ref, out_ref, back_recv).wait()


def pick(where_ref, got_ref, out_ref):
    for tile in range(2):
        def two(m, carry, tile=tile):
            a = got_ref[where_ref[tile * RH + 2 * m]].astype(jnp.float32)
            b = got_ref[where_ref[tile * RH + 2 * m + 1]].astype(jnp.float32)
            side = slice(tile * BLOCK, (tile + 1) * BLOCK)
            at = pl.multiple_of(m * SPAN, SPAN)
            out_ref[tile, :, pl.ds(at, SPAN)] = jnp.concatenate([a[:, side], b[:, side]], axis=1)
            return carry

        lax.fori_loop(0, RH // 2, two, 0)


def body(density, density_rows, square_rows, panel_shift):
    row = lax.axis_index("row")
    col = lax.axis_index("col")
    shift = lax.dynamic_slice(panel_shift, (2 * row,), (2,))
    drow = lax.dynamic_slice(density_rows, (2 * row, col, 0), (2, 1, RH)).reshape(2, RH)
    srow = lax.dynamic_slice(square_rows, (2 * row, col, 0), (2, 1, RH)).reshape(2, RH)
    channel = jnp.mod(drow - shift[:, None], PANEL)
    slots = jnp.arange(RH, 2 * RH, dtype=jnp.int32)
    match = channel[:, None, :] == jnp.arange(PANEL, dtype=jnp.int32)[None, :, None]
    source = jnp.sum(jnp.where(match, slots, 0), axis=-1).reshape(-1)
    where = jnp.mod(srow - shift[:, None], PANEL).reshape(-1)

    bf16, f32 = jnp.bfloat16, jnp.float32
    got = pl.pallas_call(
        kernel,
        out_shape=jax.ShapeDtypeStruct((PANEL, BLOCK, SPAN), bf16),
        in_specs=[
            pl.BlockSpec(memory_space=pltpu.SMEM),
            pl.BlockSpec(memory_space=pltpu.SMEM),
            pl.BlockSpec(memory_space=pltpu.VMEM),
            pl.BlockSpec(memory_space=pltpu.VMEM),
        ],
        out_specs=pl.BlockSpec(memory_space=pl.ANY),
        scratch_shapes=[
            pltpu.VMEM((RH, BLOCK, SPAN), bf16),
            pltpu.VMEM((PANEL, BLOCK, SPAN), bf16),
            pltpu.VMEM((4, N_COL, BLOCK, SPAN), bf16),
            pltpu.VMEM((FULL, FULL), bf16),
            pltpu.VMEM((HALF, FULL), f32),
            pltpu.VMEM((HALF, FULL), bf16),
            pltpu.VMEM((NPAN // 2, 8, FULL), f32),
            pltpu.VMEM((4, N_COL, BLOCK, SPAN), bf16),
            pltpu.SemaphoreType.DMA,
            pltpu.SemaphoreType.DMA((4,)),
            pltpu.SemaphoreType.DMA((4,)),
            pltpu.SemaphoreType.DMA((4,)),
            pltpu.SemaphoreType.DMA,
            pltpu.SemaphoreType.DMA,
        ],
        compiler_params=pltpu.CompilerParams(
            collective_id=0, has_side_effects=True, vmem_limit_bytes=40 * 2**20
        ),
    )(source, panel_shift, density, square_rows)
    return pl.pallas_call(
        pick,
        out_shape=jax.ShapeDtypeStruct((2, BLOCK, RH * BLOCK), f32),
        in_specs=[
            pl.BlockSpec(memory_space=pltpu.SMEM),
            pl.BlockSpec(memory_space=pltpu.VMEM),
        ],
        out_specs=pl.BlockSpec(memory_space=pltpu.VMEM),
        compiler_params=pltpu.CompilerParams(vmem_limit_bytes=16 * 2**20),
    )(where, got)


def solution(mesh):
    placed = (P("row", None, "col"), P(), P(), P())
    return jax.shard_map(
        body, mesh=mesh, in_specs=placed, out_specs=P("row", None, "col"), check_vma=False
    )
```

```python
import itertools

import jax
import jax.numpy as jnp
from jax import lax
from jax.experimental import pallas as pl
from jax.experimental.pallas import tpu as pltpu
from jax.sharding import PartitionSpec as P

PANEL = 49
BLOCK = 64
SPAN = 2 * BLOCK
RH = 32
NPAN = 16
N_ROW = 8
N_COL = 16
HALF = NPAN * BLOCK // 2
FULL = NPAN * BLOCK
MESH = pl.DeviceIdType.MESH


def wrap(value, size):
    return jnp.where(value >= size, value - size, value)


def order():
    plain = list(itertools.product(range(4), repeat=3))
    return [plain[(i * 27 + 21) % 64] for i in range(64)]


def low_high(a, b):
    low = jnp.concatenate([a[:, :BLOCK], b[:, :BLOCK]], axis=1)
    high = jnp.concatenate([a[:, BLOCK:], b[:, BLOCK:]], axis=1)
    return low, high


def kernel(
    density, drows_hbm, srows_hbm, shift_hbm, out_ref,
    x_ref, drows, srows, shift, blocks, send, recv, mat, acc, sq, mask, back,
    load_sem, send_sem, recv_sem, sib_send, sib_recv, back_send, back_recv, meet_sem,
):
    row = lax.axis_index("row")
    col = lax.axis_index("col")
    core = col % 2
    y = row % 4
    z_lo = row // 4
    x = col // 4
    z_hi = (col // 2) % 2
    z = 2 * z_hi + z_lo
    d = (x + y + z) % 4
    corner = (row + col // 2) == 0
    works = jnp.logical_or(d != 0, corner)
    mine = jnp.where(corner, PANEL - 1, (x * 4 + y) * 3 + d - 1)
    own = jnp.logical_and(works, core == z_lo)
    sibling = col + 1 - 2 * core

    loads = [
        pltpu.make_async_copy(density, x_ref, load_sem.at[0]),
        pltpu.make_async_copy(drows_hbm.at[pl.ds(2 * row, 2)], drows, load_sem.at[1]),
        pltpu.make_async_copy(shift_hbm, shift, load_sem.at[2]),
        pltpu.make_async_copy(srows_hbm.at[pl.ds(core * (NPAN // 2), NPAN // 2)], srows, load_sem.at[3]),
    ]
    for load in loads:
        load.start()

    barrier = pltpu.get_barrier_semaphore()
    for k in range(1, N_COL):
        pl.semaphore_signal(barrier, inc=1, device_id=(row, wrap(col + k, N_COL)), device_id_type=MESH)
    for k in range(1, N_ROW):
        pl.semaphore_signal(barrier, inc=1, device_id=(wrap(row + k, N_ROW), col), device_id_type=MESH)

    loads[0].wait()
    low_side = (lax.broadcasted_iota(jnp.int32, (1, SPAN), 1) < BLOCK).astype(jnp.bfloat16)
    sides = (low_side, 1 - low_side)
    for tile in range(2):
        for m in range(RH // 2):
            wide = x_ref[tile, :, m * SPAN : (m + 1) * SPAN]
            turned = jnp.concatenate([wide[:, BLOCK:], wide[:, :BLOCK]], axis=1)
            first, second = (wide, turned) if tile == 0 else (turned, wide)
            blocks[tile * (RH + 1) + 2 * m] = first * sides[tile]
            blocks[tile * (RH + 1) + 2 * m + 1] = second * sides[tile]
        blocks[tile * (RH + 1) + RH] = jnp.zeros((BLOCK, SPAN), jnp.bfloat16)

    loads[1].wait()
    loads[2].wait()
    loads[3].wait()

    pl.semaphore_wait(barrier, N_COL + N_ROW - 2)
    for k in range(1, N_ROW):
        pl.semaphore_signal(meet_sem, inc=1, device_id=(wrap(row + k, N_ROW), col), device_id_type=MESH)

    begin = []
    for tile in range(2):
        s = shift[2 * row + tile]
        e = jnp.int32(0)
        for i in range(RH):
            e = e + (drows[tile, col, i] < s).astype(jnp.int32)
        begin += [s, wrap(e, RH)]

    def fetch(u, carry):
        r0, e0, r1, e1 = carry
        hit0 = drows[0, col, e0] == r0
        hit1 = drows[1, col, e1] == r1
        send[u] = blocks[jnp.where(hit0, e0, RH)] + blocks[RH + 1 + jnp.where(hit1, e1, RH)]
        e0 = wrap(e0 + hit0.astype(jnp.int32), RH)
        e1 = wrap(e1 + hit1.astype(jnp.int32), RH)
        return wrap(r0 + 1, PANEL), e0, wrap(r1 + 1, PANEL), e1

    lax.fori_loop(0, PANEL, fetch, tuple(begin))

    pl.semaphore_wait(meet_sem, N_ROW - 1)

    xs = [wrap(x + k, 4) for k in range(4)]
    ys = [wrap(y + k, 4) for k in range(4)]

    def post(u, to_x, to_y, to_z, may_stay):
        to_row = (to_z % 2) * 4 + to_y
        to_col = to_x * 4 + (to_z // 2) * 2 + z_lo

        def remote():
            pltpu.make_async_remote_copy(
                src_ref=send.at[u],
                dst_ref=recv.at[y, col],
                send_sem=send_sem,
                recv_sem=recv_sem.at[y],
                device_id=(to_row, to_col),
                device_id_type=MESH,
            ).start()

        def local():
            pltpu.make_async_copy(send.at[u], recv.at[y, col], recv_sem.at[y]).start()

        if may_stay:
            stays = jnp.logical_and(to_row == row, to_col == col)
            pl.when(stays)(local)
            pl.when(jnp.logical_not(stays))(remote)
        else:
            remote()

    zs = [wrap(z + k, 4) for k in range(4)]
    ds = [wrap(d + k, 4) for k in range(4)]
    for dx, dy, dz in order():
        to_x, to_y, to_z, to_d = xs[dx], ys[dy], zs[dz], ds[(dx + dy + dz) % 4]
        u = jnp.where(to_d == 0, PANEL - 1, to_x * 12 + to_y * 3 + to_d - 1)

        @pl.when(jnp.logical_or(to_d != 0, (to_x + to_y + to_z) == 0))
        def _():
            post(u, to_x, to_y, to_z, dx == dy == dz == 0)

    @pl.when(works)
    def _():
        half = pl.multiple_of(core * HALF, HALF)
        there = pl.multiple_of((1 - core) * HALF, HALF)

        spread = jnp.where(
            lax.broadcasted_iota(jnp.int32, (NPAN, FULL), 1) // BLOCK
            == lax.broadcasted_iota(jnp.int32, (NPAN, FULL), 0),
            1.0,
            0.0,
        ).astype(jnp.bfloat16)
        for k in range(NPAN // 2):
            past = srows[k] - shift[core * (NPAN // 2) + k]
            hit = jnp.logical_or(past == mine, past == mine - PANEL)
            hit = jnp.where(hit, 1.0, 0.0).astype(jnp.bfloat16)
            count = lax.dot_general(
                jnp.ones((8, RH), jnp.bfloat16), hit, (((1,), (1,)), ((), ())),
                preferred_element_type=jnp.float32,
            ).astype(jnp.bfloat16)
            mask[k] = jnp.dot(count, spread, preferred_element_type=jnp.float32)

        def arrive(g, carry):
            pltpu.make_async_copy(recv.at[g], recv.at[g], recv_sem.at[g]).wait()
            base = pl.multiple_of(core * HALF + g * SPAN, SPAN)
            for c in range(N_COL // 2):
                low, high = low_high(recv[g, 2 * c], recv[g, 2 * c + 1])
                mat[pl.ds(base, BLOCK), pl.ds(c * SPAN, SPAN)] = low
                mat[pl.ds(base + BLOCK, BLOCK), pl.ds(c * SPAN, SPAN)] = high
            pltpu.make_async_remote_copy(
                src_ref=mat.at[pl.ds(base, SPAN)],
                dst_ref=mat.at[pl.ds(base, SPAN)],
                send_sem=sib_send.at[g],
                recv_sem=sib_recv.at[g],
                device_id=(row, sibling),
                device_id_type=MESH,
            ).start()
            return carry

        lax.fori_loop(0, 4, arrive, 0)

        acc[...] = jnp.dot(
            mat[pl.ds(half, HALF), pl.ds(half, HALF)],
            mat[pl.ds(half, HALF), :],
            preferred_element_type=jnp.float32,
        )

        def met(g, carry):
            sent = pl.multiple_of(half + g * SPAN, SPAN)
            came = pl.multiple_of(there + g * SPAN, SPAN)
            copy = pltpu.make_async_remote_copy(
                src_ref=mat.at[pl.ds(sent, SPAN)],
                dst_ref=mat.at[pl.ds(came, SPAN)],
                send_sem=sib_send.at[g],
                recv_sem=sib_recv.at[g],
                device_id=(row, sibling),
                device_id_type=MESH,
            )
            copy.wait_send()
            copy.wait_recv()
            return carry

        lax.fori_loop(0, 4, met, 0)

        for n in range(FULL // 256):
            at = slice(n * 256, (n + 1) * 256)
            whole = acc[:, at] + jnp.dot(
                mat[pl.ds(half, HALF), pl.ds(there, HALF)],
                mat[pl.ds(there, HALF), at],
                preferred_element_type=jnp.float32,
            )
            for k in range(NPAN // 2):
                part = slice(k * BLOCK, (k + 1) * BLOCK)
                sq[part, at] = (whole[part] * mask[k, 0:1, at]).astype(jnp.bfloat16)

        for i in (2, 1, 3, 0):
            n = xs[i]
            at = pl.multiple_of(n * 256, 256)
            cube = jnp.dot(sq[...], mat[:, pl.ds(at, 256)], preferred_element_type=jnp.float32)
            done = (3.0 * sq[:, pl.ds(at, 256)].astype(jnp.float32) - 2.0 * cube).astype(jnp.bfloat16)
            for g in range(4):
                for c in range(2):
                    top = done[g * SPAN : g * SPAN + BLOCK, c * SPAN : (c + 1) * SPAN]
                    under = done[g * SPAN + BLOCK : (g + 1) * SPAN, c * SPAN : (c + 1) * SPAN]
                    low, high = low_high(top, under)
                    back[g, 4 * n + 2 * c] = low
                    back[g, 4 * n + 2 * c + 1] = high
            for dz, dy, dc in itertools.product((1, 0), (2, 1, 3, 0), range(2)):
                g = ys[dy]
                j = 4 * n + 2 * wrap(z_hi + dz, 2) + wrap(core + dc, 2)
                to_row = 4 * core + g
                remote = jnp.logical_or(to_row != row, j != col)
                if dz == dy == dc == 0:

                    @pl.when(jnp.logical_not(remote))
                    def _():
                        pltpu.make_async_copy(back.at[g, j], out_ref.at[mine], back_recv).start()

                @pl.when(remote)
                def _():
                    pltpu.make_async_remote_copy(
                        src_ref=back.at[g, j],
                        dst_ref=out_ref.at[mine],
                        send_sem=back_send,
                        recv_sem=back_recv,
                        device_id=(to_row, j),
                        device_id_type=MESH,
                    ).start()

    @pl.when(own)
    def _():
        most = send.at[pl.ds(0, PANEL - 1)]
        pltpu.make_async_copy(most, most, send_sem).wait()

    @pl.when(jnp.logical_not(own))
    def _():
        pltpu.make_async_copy(send, send, send_sem).wait()

    @pl.when(own)
    def _():
        flat = back.reshape(4 * N_COL, BLOCK, SPAN).at[pl.ds(0, 4 * N_COL - 1)]
        pltpu.make_async_copy(flat, flat, back_send).wait()

    @pl.when(jnp.logical_and(works, jnp.logical_not(own)))
    def _():
        pltpu.make_async_copy(back, back, back_send).wait()

    pltpu.make_async_copy(out_ref, out_ref, back_recv).wait()


def pick(srows_hbm, shift_hbm, got_hbm, out_hbm, srows, shift, got_ref, out, load_sem, out_sem):
    row = lax.axis_index("row")
    col = lax.axis_index("col")
    loads = [
        pltpu.make_async_copy(srows_hbm.at[pl.ds(2 * row, 2)], srows, load_sem.at[0]),
        pltpu.make_async_copy(shift_hbm, shift, load_sem.at[1]),
        pltpu.make_async_copy(got_hbm, got_ref, load_sem.at[2]),
    ]
    for load in loads:
        load.start()
    for load in loads:
        load.wait()
    parts = []
    for tile in range(2):
        s = shift[2 * row + tile]
        side = slice(tile * BLOCK, (tile + 1) * BLOCK)
        for m in range(RH // 2):
            pair = []
            for e in (2 * m, 2 * m + 1):
                u = srows[tile, col, e] - s
                pair.append(got_ref[jnp.where(u < 0, u + PANEL, u)][:, side])
            out[tile, :, m * SPAN : (m + 1) * SPAN] = jnp.concatenate(pair, axis=1).astype(jnp.float32)
            if m % 4 == 3:
                part = (tile, slice(None), pl.ds((m - 3) * SPAN, 4 * SPAN))
                parts.append(pltpu.make_async_copy(out.at[part], out_hbm.at[part], out_sem.at[len(parts)]))
                parts[-1].start()
    for part in parts:
        part.wait()


def body(density, density_rows, square_rows, panel_shift):
    bf16, f32, i32 = jnp.bfloat16, jnp.float32, jnp.int32
    dma = pltpu.SemaphoreType.DMA
    in_hbm = pl.BlockSpec(memory_space=pltpu.HBM)
    got = pl.pallas_call(
        kernel,
        out_shape=jax.ShapeDtypeStruct((PANEL, BLOCK, SPAN), bf16),
        in_specs=[in_hbm] * 4,
        out_specs=pl.BlockSpec(memory_space=pl.ANY),
        scratch_shapes=[
            pltpu.VMEM((2, BLOCK, RH * BLOCK), bf16),
            pltpu.SMEM((2, N_COL, RH), i32),
            pltpu.VMEM((NPAN // 2, N_COL, RH), i32),
            pltpu.SMEM((NPAN,), i32),
            pltpu.VMEM((2 * (RH + 1), BLOCK, SPAN), bf16),
            pltpu.VMEM((PANEL, BLOCK, SPAN), bf16),
            pltpu.VMEM((4, N_COL, BLOCK, SPAN), bf16),
            pltpu.VMEM((FULL, FULL), bf16),
            pltpu.VMEM((HALF, FULL), f32),
            pltpu.VMEM((HALF, FULL), bf16),
            pltpu.VMEM((NPAN // 2, 8, FULL), f32),
            pltpu.VMEM((4, N_COL, BLOCK, SPAN), bf16),
            dma((4,)),
            dma,
            dma((4,)),
            dma((4,)),
            dma((4,)),
            dma,
            dma,
            pltpu.SemaphoreType.REGULAR,
        ],
        compiler_params=pltpu.CompilerParams(
            collective_id=0, has_side_effects=True, vmem_limit_bytes=60 * 2**20
        ),
    )(density, density_rows, square_rows, panel_shift)
    return pl.pallas_call(
        pick,
        out_shape=jax.ShapeDtypeStruct((2, BLOCK, RH * BLOCK), f32),
        in_specs=[in_hbm] * 3,
        out_specs=pl.BlockSpec(memory_space=pl.ANY),
        scratch_shapes=[
            pltpu.SMEM((2, N_COL, RH), i32),
            pltpu.SMEM((NPAN,), i32),
            pltpu.VMEM((PANEL, BLOCK, SPAN), bf16),
            pltpu.VMEM((2, BLOCK, RH * BLOCK), f32),
            dma((3,)),
            dma((8,)),
        ],
        compiler_params=pltpu.CompilerParams(vmem_limit_bytes=60 * 2**20),
    )(square_rows, panel_shift, got)


def solution(mesh):
    placed = (P("row", None, "col"), P(), P(), P())
    return jax.shard_map(
        body, mesh=mesh, in_specs=placed, out_specs=P("row", None, "col"), check_vma=False
    )
```

```python
import itertools

import jax
import jax.numpy as jnp
from jax import lax
from jax.experimental import pallas as pl
from jax.experimental.pallas import tpu as pltpu
from jax.sharding import PartitionSpec as P

PANEL = 49
BLOCK = 64
SPAN = 2 * BLOCK
RH = 32
NPAN = 16
N_ROW = 8
N_COL = 16
HALF = NPAN * BLOCK // 2
FULL = NPAN * BLOCK
MESH = pl.DeviceIdType.MESH


def wrap(value, size):
    return jnp.where(value >= size, value - size, value)


def order():
    plain = list(itertools.product(range(4), repeat=3))
    return [plain[(i * 27 + 21) % 64] for i in range(64)]


def low_high(a, b):
    low = jnp.concatenate([a[:, :BLOCK], b[:, :BLOCK]], axis=1)
    high = jnp.concatenate([a[:, BLOCK:], b[:, BLOCK:]], axis=1)
    return low, high


def kernel(
    density, drows_hbm, srows_hbm, shift_hbm, out_ref,
    x_ref, drows, srows, kept, shift, got, blocks, send, recv, mat, acc, sq, mask, back,
    load_sem, send_sem, recv_sem, sib_send, sib_recv, back_send, back_recv, meet_sem,
):
    row = lax.axis_index("row")
    col = lax.axis_index("col")
    core = col % 2
    y = row % 4
    z_lo = row // 4
    x = col // 4
    z_hi = (col // 2) % 2
    z = 2 * z_hi + z_lo
    d = (x + y + z) % 4
    corner = (row + col // 2) == 0
    works = jnp.logical_or(d != 0, corner)
    mine = jnp.where(corner, PANEL - 1, (x * 4 + y) * 3 + d - 1)
    own = jnp.logical_and(works, core == z_lo)
    sibling = col + 1 - 2 * core

    loads = [
        pltpu.make_async_copy(density, x_ref, load_sem.at[0]),
        pltpu.make_async_copy(drows_hbm.at[pl.ds(2 * row, 2)], drows, load_sem.at[1]),
        pltpu.make_async_copy(shift_hbm, shift, load_sem.at[2]),
        pltpu.make_async_copy(srows_hbm.at[pl.ds(core * (NPAN // 2), NPAN // 2)], srows, load_sem.at[3]),
        pltpu.make_async_copy(srows_hbm.at[pl.ds(2 * row, 2)], kept, load_sem.at[4]),
    ]
    for load in loads:
        load.start()

    barrier = pltpu.get_barrier_semaphore()
    pl.semaphore_signal(barrier, inc=1, device_id=(row, sibling), device_id_type=MESH)
    told = x % 2
    lone = jnp.logical_and(own, told == core)

    @pl.when(works)
    def _():
        chip = col // 2
        for dy in range(4):
            to_row = 4 * core + wrap(y + dy, 4)
            for k in range(N_COL // 2):
                to_col = 2 * wrap(chip + k, N_COL // 2) + told

                def tell(to_row=to_row, to_col=to_col):
                    pl.semaphore_signal(barrier, inc=1, device_id=(to_row, to_col), device_id_type=MESH)

                if dy == k == 0:
                    pl.when(jnp.logical_not(lone))(tell)
                else:
                    tell()

    loads[0].wait()
    low_side = (lax.broadcasted_iota(jnp.int32, (1, SPAN), 1) < BLOCK).astype(jnp.bfloat16)
    sides = (low_side, 1 - low_side)
    for tile in range(2):
        for m in range(RH // 2):
            wide = x_ref[tile, :, m * SPAN : (m + 1) * SPAN]
            turned = jnp.concatenate([wide[:, BLOCK:], wide[:, :BLOCK]], axis=1)
            first, second = (wide, turned) if tile == 0 else (turned, wide)
            blocks[tile * (RH + 1) + 2 * m] = first * sides[tile]
            blocks[tile * (RH + 1) + 2 * m + 1] = second * sides[tile]
        blocks[tile * (RH + 1) + RH] = jnp.zeros((BLOCK, SPAN), jnp.bfloat16)

    loads[1].wait()
    loads[2].wait()
    loads[3].wait()
    loads[4].wait()

    pl.semaphore_wait(barrier, 1 + PANEL // 2 + (1 - core) - lone.astype(jnp.int32))
    pl.semaphore_signal(meet_sem, inc=1, device_id=(row, sibling), device_id_type=MESH)

    begin = []
    for tile in range(2):
        s = shift[2 * row + tile]
        e = jnp.int32(0)
        for i in range(RH):
            e = e + (drows[tile, col, i] < s).astype(jnp.int32)
        begin += [s, wrap(e, RH)]

    def fetch(u, carry):
        r0, e0, r1, e1 = carry
        hit0 = drows[0, col, e0] == r0
        hit1 = drows[1, col, e1] == r1
        send[u] = blocks[jnp.where(hit0, e0, RH)] + blocks[RH + 1 + jnp.where(hit1, e1, RH)]
        e0 = wrap(e0 + hit0.astype(jnp.int32), RH)
        e1 = wrap(e1 + hit1.astype(jnp.int32), RH)
        return wrap(r0 + 1, PANEL), e0, wrap(r1 + 1, PANEL), e1

    lax.fori_loop(0, PANEL, fetch, tuple(begin))

    pl.semaphore_wait(meet_sem, 1)

    xs = [wrap(x + k, 4) for k in range(4)]
    ys = [wrap(y + k, 4) for k in range(4)]

    def post(u, to_x, to_y, to_z, may_stay):
        to_row = (to_z % 2) * 4 + to_y
        to_col = to_x * 4 + (to_z // 2) * 2 + z_lo

        def remote():
            pltpu.make_async_remote_copy(
                src_ref=send.at[u],
                dst_ref=recv.at[y, col],
                send_sem=send_sem,
                recv_sem=recv_sem.at[y],
                device_id=(to_row, to_col),
                device_id_type=MESH,
            ).start()

        def local():
            pltpu.make_async_copy(send.at[u], recv.at[y, col], recv_sem.at[y]).start()

        if may_stay:
            stays = jnp.logical_and(to_row == row, to_col == col)
            pl.when(stays)(local)
            pl.when(jnp.logical_not(stays))(remote)
        else:
            remote()

    zs = [wrap(z + k, 4) for k in range(4)]
    ds = [wrap(d + k, 4) for k in range(4)]
    for dx, dy, dz in order():
        to_x, to_y, to_z, to_d = xs[dx], ys[dy], zs[dz], ds[(dx + dy + dz) % 4]
        u = jnp.where(to_d == 0, PANEL - 1, to_x * 12 + to_y * 3 + to_d - 1)

        @pl.when(jnp.logical_or(to_d != 0, (to_x + to_y + to_z) == 0))
        def _():
            post(u, to_x, to_y, to_z, dx == dy == dz == 0)

    @pl.when(works)
    def _():
        half = pl.multiple_of(core * HALF, HALF)
        there = pl.multiple_of((1 - core) * HALF, HALF)

        spread = jnp.where(
            lax.broadcasted_iota(jnp.int32, (NPAN, FULL), 1) // BLOCK
            == lax.broadcasted_iota(jnp.int32, (NPAN, FULL), 0),
            1.0,
            0.0,
        ).astype(jnp.bfloat16)
        for k in range(NPAN // 2):
            past = srows[k] - shift[core * (NPAN // 2) + k]
            hit = jnp.logical_or(past == mine, past == mine - PANEL)
            hit = jnp.where(hit, 1.0, 0.0).astype(jnp.bfloat16)
            count = lax.dot_general(
                jnp.ones((8, RH), jnp.bfloat16), hit, (((1,), (1,)), ((), ())),
                preferred_element_type=jnp.float32,
            ).astype(jnp.bfloat16)
            mask[k] = jnp.dot(count, spread, preferred_element_type=jnp.float32)

        def arrive(g, carry):
            pltpu.make_async_copy(recv.at[g], recv.at[g], recv_sem.at[g]).wait()
            base = pl.multiple_of(core * HALF + g * SPAN, SPAN)
            for c in range(N_COL // 2):
                low, high = low_high(recv[g, 2 * c], recv[g, 2 * c + 1])
                mat[pl.ds(base, BLOCK), pl.ds(c * SPAN, SPAN)] = low
                mat[pl.ds(base + BLOCK, BLOCK), pl.ds(c * SPAN, SPAN)] = high
            pltpu.make_async_remote_copy(
                src_ref=mat.at[pl.ds(base, SPAN)],
                dst_ref=mat.at[pl.ds(base, SPAN)],
                send_sem=sib_send.at[g],
                recv_sem=sib_recv.at[g],
                device_id=(row, sibling),
                device_id_type=MESH,
            ).start()
            return carry

        lax.fori_loop(0, 4, arrive, 0)

        acc[...] = jnp.dot(
            mat[pl.ds(half, HALF), pl.ds(half, HALF)],
            mat[pl.ds(half, HALF), :],
            preferred_element_type=jnp.float32,
        )

        def met(g, carry):
            sent = pl.multiple_of(half + g * SPAN, SPAN)
            came = pl.multiple_of(there + g * SPAN, SPAN)
            copy = pltpu.make_async_remote_copy(
                src_ref=mat.at[pl.ds(sent, SPAN)],
                dst_ref=mat.at[pl.ds(came, SPAN)],
                send_sem=sib_send.at[g],
                recv_sem=sib_recv.at[g],
                device_id=(row, sibling),
                device_id_type=MESH,
            )
            copy.wait_send()
            copy.wait_recv()
            return carry

        lax.fori_loop(0, 4, met, 0)

        for n in range(FULL // 256):
            at = slice(n * 256, (n + 1) * 256)
            whole = acc[:, at] + jnp.dot(
                mat[pl.ds(half, HALF), pl.ds(there, HALF)],
                mat[pl.ds(there, HALF), at],
                preferred_element_type=jnp.float32,
            )
            for k in range(NPAN // 2):
                part = slice(k * BLOCK, (k + 1) * BLOCK)
                sq[part, at] = (whole[part] * mask[k, 0:1, at]).astype(jnp.bfloat16)

        def give(n, to_z, may_stay):
            for dy, to_core in itertools.product((2, 1, 3, 0), range(2)):
                g = ys[dy]
                j = 4 * n + 2 * to_z + to_core
                to_row = 4 * core + g

                def remote(g=g, j=j, to_row=to_row):
                    pltpu.make_async_remote_copy(
                        src_ref=back.at[g, j],
                        dst_ref=got.at[mine],
                        send_sem=back_send,
                        recv_sem=back_recv,
                        device_id=(to_row, j),
                        device_id_type=MESH,
                    ).start()

                def local(g=g, j=j):
                    pltpu.make_async_copy(back.at[g, j], got.at[mine], back_recv).start()

                if may_stay and dy == 0:
                    stays = jnp.logical_and(to_row == row, j == col)
                    pl.when(stays)(local)
                    pl.when(jnp.logical_not(stays))(remote)
                else:
                    remote()

        for k, i in enumerate((2, 1, 3, 0)):
            n = xs[i]
            at = pl.multiple_of(n * 256, 256)
            cube = jnp.dot(sq[...], mat[:, pl.ds(at, 256)], preferred_element_type=jnp.float32)
            done = (3.0 * sq[:, pl.ds(at, 256)].astype(jnp.float32) - 2.0 * cube).astype(jnp.bfloat16)
            for g in range(4):
                for c in range(2):
                    top = done[g * SPAN : g * SPAN + BLOCK, c * SPAN : (c + 1) * SPAN]
                    under = done[g * SPAN + BLOCK : (g + 1) * SPAN, c * SPAN : (c + 1) * SPAN]
                    low, high = low_high(top, under)
                    back[g, 4 * n + 2 * c] = low
                    back[g, 4 * n + 2 * c + 1] = high
            give(n, 0, i == 0)
            give(n, 1, i == 0)

    @pl.when(own)
    def _():
        most = send.at[pl.ds(0, PANEL - 1)]
        pltpu.make_async_copy(most, most, send_sem).wait()

    @pl.when(jnp.logical_not(own))
    def _():
        pltpu.make_async_copy(send, send, send_sem).wait()

    @pl.when(own)
    def _():
        flat = back.reshape(4 * N_COL, BLOCK, SPAN).at[pl.ds(0, 4 * N_COL - 1)]
        pltpu.make_async_copy(flat, flat, back_send).wait()

    @pl.when(jnp.logical_and(works, jnp.logical_not(own)))
    def _():
        pltpu.make_async_copy(back, back, back_send).wait()

    pltpu.make_async_copy(got, got, back_recv).wait()
    for tile in range(2):
        s = shift[2 * row + tile]
        side = slice(tile * BLOCK, (tile + 1) * BLOCK)
        for m in range(RH // 2):
            pair = []
            for e in (2 * m, 2 * m + 1):
                u = kept[tile, col, e] - s
                pair.append(got[jnp.where(u < 0, u + PANEL, u)][:, side])
            out_ref[tile, :, m * SPAN : (m + 1) * SPAN] = jnp.concatenate(pair, axis=1).astype(jnp.float32)


def body(density, density_rows, square_rows, panel_shift):
    bf16, f32, i32 = jnp.bfloat16, jnp.float32, jnp.int32
    dma = pltpu.SemaphoreType.DMA
    in_hbm = pl.BlockSpec(memory_space=pltpu.HBM)
    density, density_rows, square_rows, panel_shift = [
        pltpu.with_memory_space_constraint(v, pltpu.HBM)
        for v in (density, density_rows, square_rows, panel_shift)
    ]
    return pl.pallas_call(
        kernel,
        out_shape=jax.ShapeDtypeStruct((2, BLOCK, RH * BLOCK), f32),
        in_specs=[in_hbm] * 4,
        out_specs=pl.BlockSpec(memory_space=pltpu.VMEM),
        scratch_shapes=[
            pltpu.VMEM((2, BLOCK, RH * BLOCK), bf16),
            pltpu.SMEM((2, N_COL, RH), i32),
            pltpu.VMEM((NPAN // 2, N_COL, RH), i32),
            pltpu.SMEM((2, N_COL, RH), i32),
            pltpu.SMEM((NPAN,), i32),
            pltpu.VMEM((PANEL, BLOCK, SPAN), bf16),
            pltpu.VMEM((2 * (RH + 1), BLOCK, SPAN), bf16),
            pltpu.VMEM((PANEL, BLOCK, SPAN), bf16),
            pltpu.VMEM((4, N_COL, BLOCK, SPAN), bf16),
            pltpu.VMEM((FULL, FULL), bf16),
            pltpu.VMEM((HALF, FULL), f32),
            pltpu.VMEM((HALF, FULL), bf16),
            pltpu.VMEM((NPAN // 2, 8, FULL), f32),
            pltpu.VMEM((4, N_COL, BLOCK, SPAN), bf16),
            dma((5,)),
            dma,
            dma((4,)),
            dma((4,)),
            dma((4,)),
            dma,
            dma,
            pltpu.SemaphoreType.REGULAR,
        ],
        compiler_params=pltpu.CompilerParams(
            collective_id=0, has_side_effects=True, vmem_limit_bytes=40 * 2**20
        ),
    )(density, density_rows, square_rows, panel_shift)


def solution(mesh):
    placed = (P("row", None, "col"), P(), P(), P())
    return jax.shard_map(
        body, mesh=mesh, in_specs=placed, out_specs=P("row", None, "col"), check_vma=False
    )
```

```python
import itertools

import jax
import jax.numpy as jnp
from jax import lax
from jax.experimental import pallas as pl
from jax.experimental.pallas import tpu as pltpu
from jax.sharding import PartitionSpec as P

PANEL = 49
BLOCK = 64
SPAN = 2 * BLOCK
RH = 32
NPAN = 16
N_ROW = 8
N_COL = 16
HALF = NPAN * BLOCK // 2
FULL = NPAN * BLOCK
MESH = pl.DeviceIdType.MESH


def wrap(value, size):
    return jnp.where(value >= size, value - size, value)


def order():
    plain = list(itertools.product(range(4), repeat=3))
    return [plain[(i * 27 + 21) % 64] for i in range(64)]


def low_high(a, b):
    low = jnp.concatenate([a[:, :BLOCK], b[:, :BLOCK]], axis=1)
    high = jnp.concatenate([a[:, BLOCK:], b[:, BLOCK:]], axis=1)
    return low, high


def kernel(
    density, drows_hbm, srows_hbm, shift_hbm, out_ref,
    x_ref, drows, srows, kept, shift, got, blocks, send, recv, mat, acc, sq, mask, back,
    load_sem, send_sem, recv_sem, sib_send, sib_recv, back_send, back_recv, meet_sem,
):
    row = lax.axis_index("row")
    col = lax.axis_index("col")
    core = col % 2
    y = row % 4
    z_lo = row // 4
    x = col // 4
    z_hi = (col // 2) % 2
    z = 2 * z_hi + z_lo
    d = (x + y + z) % 4
    corner = (row + col // 2) == 0
    works = jnp.logical_or(d != 0, corner)
    mine = jnp.where(corner, PANEL - 1, (x * 4 + y) * 3 + d - 1)
    own = jnp.logical_and(works, core == z_lo)
    sibling = col + 1 - 2 * core

    loads = [
        pltpu.make_async_copy(density, x_ref, load_sem.at[0]),
        pltpu.make_async_copy(drows_hbm.at[pl.ds(2 * row, 2)], drows, load_sem.at[1]),
        pltpu.make_async_copy(shift_hbm, shift, load_sem.at[2]),
        pltpu.make_async_copy(srows_hbm.at[pl.ds(core * (NPAN // 2), NPAN // 2)], srows, load_sem.at[3]),
        pltpu.make_async_copy(srows_hbm.at[pl.ds(2 * row, 2)], kept, load_sem.at[4]),
    ]
    for load in loads:
        load.start()

    barrier = pltpu.get_barrier_semaphore()
    pl.semaphore_signal(barrier, inc=1, device_id=(row, sibling), device_id_type=MESH)
    told = x % 2
    lone = jnp.logical_and(own, told == core)

    @pl.when(works)
    def _():
        chip = col // 2
        for dy in range(4):
            to_row = 4 * core + wrap(y + dy, 4)
            for k in range(N_COL // 2):
                to_col = 2 * wrap(chip + k, N_COL // 2) + told

                def tell(to_row=to_row, to_col=to_col):
                    pl.semaphore_signal(barrier, inc=1, device_id=(to_row, to_col), device_id_type=MESH)

                if dy == k == 0:
                    pl.when(jnp.logical_not(lone))(tell)
                else:
                    tell()

    loads[0].wait()
    low_side = (lax.broadcasted_iota(jnp.int32, (1, SPAN), 1) < BLOCK).astype(jnp.bfloat16)
    sides = (low_side, 1 - low_side)
    for tile in range(2):
        for m in range(RH // 2):
            wide = x_ref[tile, :, m * SPAN : (m + 1) * SPAN]
            turned = jnp.concatenate([wide[:, BLOCK:], wide[:, :BLOCK]], axis=1)
            first, second = (wide, turned) if tile == 0 else (turned, wide)
            blocks[tile * (RH + 1) + 2 * m] = first * sides[tile]
            blocks[tile * (RH + 1) + 2 * m + 1] = second * sides[tile]
        blocks[tile * (RH + 1) + RH] = jnp.zeros((BLOCK, SPAN), jnp.bfloat16)

    loads[1].wait()
    loads[2].wait()
    loads[3].wait()
    loads[4].wait()

    pl.semaphore_wait(barrier, 1 + PANEL // 2 + (1 - core) - lone.astype(jnp.int32))
    pl.semaphore_signal(meet_sem, inc=1, device_id=(row, sibling), device_id_type=MESH)

    begin = []
    for tile in range(2):
        s = shift[2 * row + tile]
        e = jnp.int32(0)
        for i in range(RH):
            e = e + (drows[tile, col, i] < s).astype(jnp.int32)
        begin += [s, wrap(e, RH)]

    def fetch(u, carry):
        r0, e0, r1, e1 = carry
        hit0 = drows[0, col, e0] == r0
        hit1 = drows[1, col, e1] == r1
        send[u] = blocks[jnp.where(hit0, e0, RH)] + blocks[RH + 1 + jnp.where(hit1, e1, RH)]
        e0 = wrap(e0 + hit0.astype(jnp.int32), RH)
        e1 = wrap(e1 + hit1.astype(jnp.int32), RH)
        return wrap(r0 + 1, PANEL), e0, wrap(r1 + 1, PANEL), e1

    lax.fori_loop(0, PANEL, fetch, tuple(begin))

    pl.semaphore_wait(meet_sem, 1)

    xs = [wrap(x + k, 4) for k in range(4)]
    ys = [wrap(y + k, 4) for k in range(4)]

    def post(u, to_x, to_y, to_z, place, may_stay):
        slot = recv.at[place // 8, place % 8 // 2, core]
        arrived = recv_sem.at[place // 8]
        to_row = (to_z % 2) * 4 + to_y
        to_col = to_x * 4 + (to_z // 2) * 2 + z_lo

        def remote():
            pltpu.make_async_remote_copy(
                src_ref=send.at[u],
                dst_ref=slot,
                send_sem=send_sem,
                recv_sem=arrived,
                device_id=(to_row, to_col),
                device_id_type=MESH,
            ).start()

        def local():
            pltpu.make_async_copy(send.at[u], slot, arrived).start()

        if may_stay:
            stays = jnp.logical_and(to_row == row, to_col == col)
            pl.when(stays)(local)
            pl.when(jnp.logical_not(stays))(remote)
        else:
            remote()

    zs = [wrap(z + k, 4) for k in range(4)]
    ds = [wrap(d + k, 4) for k in range(4)]
    for place, (dx, dy, dz) in enumerate(order()):
        to_x, to_y, to_z, to_d = xs[dx], ys[dy], zs[dz], ds[(dx + dy + dz) % 4]
        u = jnp.where(to_d == 0, PANEL - 1, to_x * 12 + to_y * 3 + to_d - 1)

        @pl.when(jnp.logical_or(to_d != 0, (to_x + to_y + to_z) == 0))
        def _():
            post(u, to_x, to_y, to_z, place, dx == dy == dz == 0)

    @pl.when(works)
    def _():
        half = pl.multiple_of(core * HALF, HALF)
        there = pl.multiple_of((1 - core) * HALF, HALF)

        spread = jnp.where(
            lax.broadcasted_iota(jnp.int32, (NPAN, FULL), 1) // BLOCK
            == lax.broadcasted_iota(jnp.int32, (NPAN, FULL), 0),
            1.0,
            0.0,
        ).astype(jnp.bfloat16)
        for k in range(NPAN // 2):
            past = srows[k] - shift[core * (NPAN // 2) + k]
            hit = jnp.logical_or(past == mine, past == mine - PANEL)
            hit = jnp.where(hit, 1.0, 0.0).astype(jnp.bfloat16)
            count = lax.dot_general(
                jnp.ones((8, RH), jnp.bfloat16), hit, (((1,), (1,)), ((), ())),
                preferred_element_type=jnp.float32,
            ).astype(jnp.bfloat16)
            mask[k] = jnp.dot(count, spread, preferred_element_type=jnp.float32)

        straight = core == z_lo
        offsets = order()
        for k in range(8):
            pltpu.make_async_copy(recv.at[k], recv.at[k], recv_sem.at[k]).wait()
            for j in range(4):
                even, odd = sorted(offsets[8 * k + 2 * j : 8 * k + 2 * j + 2], key=lambda offset: offset[2] % 2)
                dx, dy, dz = (jnp.where(straight, one, other) for one, other in zip(even, odd))
                from_x, from_y, from_z = wrap(x + 4 - dx, 4), wrap(y + 4 - dy, 4), wrap(z + 4 - dz, 4)
                base = pl.multiple_of(core * HALF + from_y * SPAN, SPAN)
                at = pl.multiple_of((from_x * 2 + from_z // 2) * SPAN, SPAN)
                low, high = low_high(recv[k, j, 0], recv[k, j, 1])
                mat[pl.ds(base, BLOCK), pl.ds(at, SPAN)] = low
                mat[pl.ds(base + BLOCK, BLOCK), pl.ds(at, SPAN)] = high
                square = mat.at[pl.ds(base, SPAN), pl.ds(at, SPAN)]
                pltpu.make_async_remote_copy(
                    src_ref=square,
                    dst_ref=square,
                    send_sem=sib_send,
                    recv_sem=sib_recv,
                    device_id=(row, sibling),
                    device_id_type=MESH,
                ).start()

        acc[...] = jnp.dot(
            mat[pl.ds(half, HALF), pl.ds(half, HALF)],
            mat[pl.ds(half, HALF), :],
            preferred_element_type=jnp.float32,
        )

        came = mat.at[pl.ds(there, HALF)]
        pltpu.make_async_copy(came, came, sib_recv).wait()

        for n in range(FULL // 256):
            at = slice(n * 256, (n + 1) * 256)
            whole = acc[:, at] + jnp.dot(
                mat[pl.ds(half, HALF), pl.ds(there, HALF)],
                mat[pl.ds(there, HALF), at],
                preferred_element_type=jnp.float32,
            )
            for k in range(NPAN // 2):
                part = slice(k * BLOCK, (k + 1) * BLOCK)
                sq[part, at] = (whole[part] * mask[k, 0:1, at]).astype(jnp.bfloat16)

        def give(n, to_z, may_stay):
            for dy, dc in itertools.product((2, 1, 3, 0), range(2)):
                to_core = wrap(core + dc, 2)
                g = ys[dy]
                j = 4 * n + 2 * to_z + to_core
                to_row = 4 * core + g

                def remote(g=g, j=j, to_row=to_row):
                    pltpu.make_async_remote_copy(
                        src_ref=back.at[g, j],
                        dst_ref=got.at[mine],
                        send_sem=back_send,
                        recv_sem=back_recv,
                        device_id=(to_row, j),
                        device_id_type=MESH,
                    ).start()

                def local(g=g, j=j):
                    pltpu.make_async_copy(back.at[g, j], got.at[mine], back_recv).start()

                if may_stay and dy == 0:
                    stays = jnp.logical_and(to_row == row, j == col)
                    pl.when(stays)(local)
                    pl.when(jnp.logical_not(stays))(remote)
                else:
                    remote()

        for k, i in enumerate((2, 1, 3, 0)):
            n = xs[i]
            at = pl.multiple_of(n * 256, 256)
            cube = jnp.dot(sq[...], mat[:, pl.ds(at, 256)], preferred_element_type=jnp.float32)
            done = (3.0 * sq[:, pl.ds(at, 256)].astype(jnp.float32) - 2.0 * cube).astype(jnp.bfloat16)
            for g in range(4):
                for c in range(2):
                    top = done[g * SPAN : g * SPAN + BLOCK, c * SPAN : (c + 1) * SPAN]
                    under = done[g * SPAN + BLOCK : (g + 1) * SPAN, c * SPAN : (c + 1) * SPAN]
                    low, high = low_high(top, under)
                    back[g, 4 * n + 2 * c] = low
                    back[g, 4 * n + 2 * c + 1] = high
            give(n, 1 - z_hi, i == 0)
            give(n, z_hi, i == 0)

        went = mat.at[pl.ds(half, HALF)]
        pltpu.make_async_copy(went, went, sib_send).wait()

    @pl.when(own)
    def _():
        most = send.at[pl.ds(0, PANEL - 1)]
        pltpu.make_async_copy(most, most, send_sem).wait()

    @pl.when(jnp.logical_not(own))
    def _():
        pltpu.make_async_copy(send, send, send_sem).wait()

    @pl.when(own)
    def _():
        flat = back.reshape(4 * N_COL, BLOCK, SPAN).at[pl.ds(0, 4 * N_COL - 1)]
        pltpu.make_async_copy(flat, flat, back_send).wait()

    @pl.when(jnp.logical_and(works, jnp.logical_not(own)))
    def _():
        pltpu.make_async_copy(back, back, back_send).wait()

    pltpu.make_async_copy(got, got, back_recv).wait()
    for tile in range(2):
        s = shift[2 * row + tile]
        side = slice(tile * BLOCK, (tile + 1) * BLOCK)
        for m in range(RH // 2):
            pair = []
            for e in (2 * m, 2 * m + 1):
                u = kept[tile, col, e] - s
                pair.append(got[jnp.where(u < 0, u + PANEL, u)][:, side])
            out_ref[tile, :, m * SPAN : (m + 1) * SPAN] = jnp.concatenate(pair, axis=1).astype(jnp.float32)


def body(density, density_rows, square_rows, panel_shift):
    bf16, f32, i32 = jnp.bfloat16, jnp.float32, jnp.int32
    dma = pltpu.SemaphoreType.DMA
    in_hbm = pl.BlockSpec(memory_space=pltpu.HBM)
    density, density_rows, square_rows, panel_shift = [
        pltpu.with_memory_space_constraint(v, pltpu.HBM)
        for v in (density, density_rows, square_rows, panel_shift)
    ]
    return pl.pallas_call(
        kernel,
        out_shape=jax.ShapeDtypeStruct((2, BLOCK, RH * BLOCK), f32),
        in_specs=[in_hbm] * 4,
        out_specs=pl.BlockSpec(memory_space=pltpu.VMEM),
        scratch_shapes=[
            pltpu.VMEM((2, BLOCK, RH * BLOCK), bf16),
            pltpu.SMEM((2, N_COL, RH), i32),
            pltpu.VMEM((NPAN // 2, N_COL, RH), i32),
            pltpu.SMEM((2, N_COL, RH), i32),
            pltpu.SMEM((NPAN,), i32),
            pltpu.VMEM((PANEL, BLOCK, SPAN), bf16),
            pltpu.VMEM((2 * (RH + 1), BLOCK, SPAN), bf16),
            pltpu.VMEM((PANEL, BLOCK, SPAN), bf16),
            pltpu.VMEM((8, 4, 2, BLOCK, SPAN), bf16),
            pltpu.VMEM((FULL, FULL), bf16),
            pltpu.VMEM((HALF, FULL), f32),
            pltpu.VMEM((HALF, FULL), bf16),
            pltpu.VMEM((NPAN // 2, 8, FULL), f32),
            pltpu.VMEM((4, N_COL, BLOCK, SPAN), bf16),
            dma((5,)),
            dma,
            dma((8,)),
            dma,
            dma,
            dma,
            dma,
            pltpu.SemaphoreType.REGULAR,
        ],
        compiler_params=pltpu.CompilerParams(
            collective_id=0, has_side_effects=True, vmem_limit_bytes=40 * 2**20
        ),
    )(density, density_rows, square_rows, panel_shift)


def solution(mesh):
    placed = (P("row", None, "col"), P(), P(), P())
    return jax.shard_map(
        body, mesh=mesh, in_specs=placed, out_specs=P("row", None, "col"), check_vma=False
    )
```

```python
import itertools

import jax
import jax.numpy as jnp
from jax import lax
from jax.experimental import pallas as pl
from jax.experimental.pallas import tpu as pltpu
from jax.sharding import PartitionSpec as P

PANEL = 49
BLOCK = 64
SPAN = 2 * BLOCK
RH = 32
NPAN = 16
N_ROW = 8
N_COL = 16
HALF = NPAN * BLOCK // 2
FULL = NPAN * BLOCK
MESH = pl.DeviceIdType.MESH


def wrap(value, size):
    return jnp.where(value >= size, value - size, value)


def order():
    plain = list(itertools.product(range(4), repeat=3))
    return [plain[(i * 27 + 21) % 64] for i in range(64)]


def low_high(a, b):
    low = jnp.concatenate([a[:, :BLOCK], b[:, :BLOCK]], axis=1)
    high = jnp.concatenate([a[:, BLOCK:], b[:, BLOCK:]], axis=1)
    return low, high


def kernel(
    density, drows_hbm, srows_hbm, shift_hbm, out_ref,
    x_ref, drows, srows, kept, shift, got, blocks, send, recv, mat, acc, sq, mask, back,
    load_sem, send_sem, recv_sem, sib_send, sib_recv, back_send, back_recv, meet_sem,
):
    row = lax.axis_index("row")
    col = lax.axis_index("col")
    core = col % 2
    y = row % 4
    z_lo = row // 4
    x = col // 4
    z_hi = (col // 2) % 2
    z = 2 * z_hi + z_lo
    d = (x + y + z) % 4
    corner = (row + col // 2) == 0
    works = jnp.logical_or(d != 0, corner)
    mine = jnp.where(corner, PANEL - 1, (x * 4 + y) * 3 + d - 1)
    own = jnp.logical_and(works, core == z_lo)
    sibling = col + 1 - 2 * core

    loads = [
        pltpu.make_async_copy(density, x_ref, load_sem.at[0]),
        pltpu.make_async_copy(drows_hbm.at[pl.ds(2 * row, 2)], drows, load_sem.at[1]),
        pltpu.make_async_copy(shift_hbm, shift, load_sem.at[2]),
        pltpu.make_async_copy(srows_hbm.at[pl.ds(core * (NPAN // 2), NPAN // 2)], srows, load_sem.at[3]),
        pltpu.make_async_copy(srows_hbm.at[pl.ds(2 * row, 2)], kept, load_sem.at[4]),
    ]
    for load in loads:
        load.start()

    barrier = pltpu.get_barrier_semaphore()
    pl.semaphore_signal(barrier, inc=1, device_id=(row, sibling), device_id_type=MESH)
    told = x % 2
    lone = jnp.logical_and(own, told == core)

    @pl.when(works)
    def _():
        chip = col // 2
        for dy in range(4):
            to_row = 4 * core + wrap(y + dy, 4)
            for k in range(N_COL // 2):
                to_col = 2 * wrap(chip + k, N_COL // 2) + told

                def tell(to_row=to_row, to_col=to_col):
                    pl.semaphore_signal(barrier, inc=1, device_id=(to_row, to_col), device_id_type=MESH)

                if dy == k == 0:
                    pl.when(jnp.logical_not(lone))(tell)
                else:
                    tell()

    loads[0].wait()
    low_side = (lax.broadcasted_iota(jnp.int32, (1, SPAN), 1) < BLOCK).astype(jnp.bfloat16)
    sides = (low_side, 1 - low_side)
    for tile in range(2):
        for m in range(RH // 2):
            wide = x_ref[tile, :, m * SPAN : (m + 1) * SPAN]
            turned = jnp.concatenate([wide[:, BLOCK:], wide[:, :BLOCK]], axis=1)
            first, second = (wide, turned) if tile == 0 else (turned, wide)
            blocks[tile * (RH + 1) + 2 * m] = first * sides[tile]
            blocks[tile * (RH + 1) + 2 * m + 1] = second * sides[tile]
        blocks[tile * (RH + 1) + RH] = jnp.zeros((BLOCK, SPAN), jnp.bfloat16)

    loads[1].wait()
    loads[2].wait()
    loads[3].wait()
    loads[4].wait()

    begin = []
    for tile in range(2):
        s = shift[2 * row + tile]
        e = jnp.int32(0)
        for i in range(RH):
            e = e + (drows[tile, col, i] < s).astype(jnp.int32)
        begin += [s, wrap(e, RH)]

    pl.semaphore_wait(barrier, 1 + PANEL // 2 + (1 - core) - lone.astype(jnp.int32))
    pl.semaphore_signal(meet_sem, inc=1, device_id=(row, sibling), device_id_type=MESH)

    def fetch(u, carry):
        r0, e0, r1, e1 = carry
        hit0 = drows[0, col, e0] == r0
        hit1 = drows[1, col, e1] == r1
        send[u] = blocks[jnp.where(hit0, e0, RH)] + blocks[RH + 1 + jnp.where(hit1, e1, RH)]
        e0 = wrap(e0 + hit0.astype(jnp.int32), RH)
        e1 = wrap(e1 + hit1.astype(jnp.int32), RH)
        return wrap(r0 + 1, PANEL), e0, wrap(r1 + 1, PANEL), e1

    lax.fori_loop(0, PANEL, fetch, tuple(begin))

    pl.semaphore_wait(meet_sem, 1)

    xs = [wrap(x + k, 4) for k in range(4)]
    ys = [wrap(y + k, 4) for k in range(4)]

    def post(u, to_x, to_y, to_z, place, may_stay):
        slot = recv.at[place // 8, place % 8 // 2, core]
        arrived = recv_sem.at[place // 8]
        to_row = (to_z % 2) * 4 + to_y
        to_col = to_x * 4 + (to_z // 2) * 2 + z_lo

        def remote():
            pltpu.make_async_remote_copy(
                src_ref=send.at[u],
                dst_ref=slot,
                send_sem=send_sem,
                recv_sem=arrived,
                device_id=(to_row, to_col),
                device_id_type=MESH,
            ).start()

        def local():
            pltpu.make_async_copy(send.at[u], slot, arrived).start()

        if may_stay:
            stays = jnp.logical_and(to_row == row, to_col == col)
            pl.when(stays)(local)
            pl.when(jnp.logical_not(stays))(remote)
        else:
            remote()

    zs = [wrap(z + k, 4) for k in range(4)]
    ds = [wrap(d + k, 4) for k in range(4)]
    for place, (dx, dy, dz) in enumerate(order()):
        to_x, to_y, to_z, to_d = xs[dx], ys[dy], zs[dz], ds[(dx + dy + dz) % 4]
        u = jnp.where(to_d == 0, PANEL - 1, to_x * 12 + to_y * 3 + to_d - 1)

        @pl.when(jnp.logical_or(to_d != 0, (to_x + to_y + to_z) == 0))
        def _():
            post(u, to_x, to_y, to_z, place, dx == dy == dz == 0)

    @pl.when(works)
    def _():
        half = pl.multiple_of(core * HALF, HALF)
        there = pl.multiple_of((1 - core) * HALF, HALF)

        spread = jnp.where(
            lax.broadcasted_iota(jnp.int32, (NPAN, FULL), 1) // BLOCK
            == lax.broadcasted_iota(jnp.int32, (NPAN, FULL), 0),
            1.0,
            0.0,
        ).astype(jnp.bfloat16)
        for k in range(NPAN // 2):
            past = srows[k] - shift[core * (NPAN // 2) + k]
            hit = jnp.logical_or(past == mine, past == mine - PANEL)
            hit = jnp.where(hit, 1.0, 0.0).astype(jnp.bfloat16)
            count = lax.dot_general(
                jnp.ones((8, RH), jnp.bfloat16), hit, (((1,), (1,)), ((), ())),
                preferred_element_type=jnp.float32,
            ).astype(jnp.bfloat16)
            mask[k] = jnp.dot(count, spread, preferred_element_type=jnp.float32)

        straight = core == z_lo
        offsets = order()
        for k in range(8):
            pltpu.make_async_copy(recv.at[k], recv.at[k], recv_sem.at[k]).wait()
            for j in range(4):
                even, odd = sorted(offsets[8 * k + 2 * j : 8 * k + 2 * j + 2], key=lambda offset: offset[2] % 2)
                dx, dy, dz = (jnp.where(straight, one, other) for one, other in zip(even, odd))
                from_x, from_y, from_z = wrap(x + 4 - dx, 4), wrap(y + 4 - dy, 4), wrap(z + 4 - dz, 4)
                base = pl.multiple_of(core * HALF + from_y * SPAN, SPAN)
                at = pl.multiple_of((from_x * 2 + from_z // 2) * SPAN, SPAN)
                low, high = low_high(recv[k, j, 0], recv[k, j, 1])
                mat[pl.ds(base, BLOCK), pl.ds(at, SPAN)] = low
                mat[pl.ds(base + BLOCK, BLOCK), pl.ds(at, SPAN)] = high
                square = mat.at[pl.ds(base, SPAN), pl.ds(at, SPAN)]
                pltpu.make_async_remote_copy(
                    src_ref=square,
                    dst_ref=square,
                    send_sem=sib_send,
                    recv_sem=sib_recv,
                    device_id=(row, sibling),
                    device_id_type=MESH,
                ).start()

        acc[...] = jnp.dot(
            mat[pl.ds(half, HALF), pl.ds(half, HALF)],
            mat[pl.ds(half, HALF), :],
            preferred_element_type=jnp.float32,
        )

        came = mat.at[pl.ds(there, HALF)]
        pltpu.make_async_copy(came, came, sib_recv).wait()

        for n in range(FULL // 256):
            at = slice(n * 256, (n + 1) * 256)
            whole = acc[:, at] + jnp.dot(
                mat[pl.ds(half, HALF), pl.ds(there, HALF)],
                mat[pl.ds(there, HALF), at],
                preferred_element_type=jnp.float32,
            )
            for k in range(NPAN // 2):
                part = slice(k * BLOCK, (k + 1) * BLOCK)
                sq[part, at] = (whole[part] * mask[k, 0:1, at]).astype(jnp.bfloat16)

        def give(n, to_z, may_stay):
            for dy, dc in itertools.product((2, 1, 3, 0), range(2)):
                to_core = wrap(core + dc, 2)
                g = ys[dy]
                j = 4 * n + 2 * to_z + to_core
                to_row = 4 * core + g

                def remote(g=g, j=j, to_row=to_row):
                    pltpu.make_async_remote_copy(
                        src_ref=back.at[g, j],
                        dst_ref=got.at[mine],
                        send_sem=back_send,
                        recv_sem=back_recv,
                        device_id=(to_row, j),
                        device_id_type=MESH,
                    ).start()

                def local(g=g, j=j):
                    pltpu.make_async_copy(back.at[g, j], got.at[mine], back_recv).start()

                if may_stay and dy == 0:
                    stays = jnp.logical_and(to_row == row, j == col)
                    pl.when(stays)(local)
                    pl.when(jnp.logical_not(stays))(remote)
                else:
                    remote()

        for k, i in enumerate((2, 1, 3, 0)):
            n = xs[i]
            at = pl.multiple_of(n * 256, 256)
            cube = jnp.dot(sq[...], mat[:, pl.ds(at, 256)], preferred_element_type=jnp.float32)
            done = (3.0 * sq[:, pl.ds(at, 256)].astype(jnp.float32) - 2.0 * cube).astype(jnp.bfloat16)
            for g in range(4):
                for c in range(2):
                    top = done[g * SPAN : g * SPAN + BLOCK, c * SPAN : (c + 1) * SPAN]
                    under = done[g * SPAN + BLOCK : (g + 1) * SPAN, c * SPAN : (c + 1) * SPAN]
                    low, high = low_high(top, under)
                    back[g, 4 * n + 2 * c] = low
                    back[g, 4 * n + 2 * c + 1] = high
            give(n, 1 - z_hi, i == 0)
            give(n, z_hi, i == 0)

        went = mat.at[pl.ds(half, HALF)]
        pltpu.make_async_copy(went, went, sib_send).wait()

    @pl.when(own)
    def _():
        most = send.at[pl.ds(0, PANEL - 1)]
        pltpu.make_async_copy(most, most, send_sem).wait()

    @pl.when(jnp.logical_not(own))
    def _():
        pltpu.make_async_copy(send, send, send_sem).wait()

    @pl.when(own)
    def _():
        flat = back.reshape(4 * N_COL, BLOCK, SPAN).at[pl.ds(0, 4 * N_COL - 1)]
        pltpu.make_async_copy(flat, flat, back_send).wait()

    @pl.when(jnp.logical_and(works, jnp.logical_not(own)))
    def _():
        pltpu.make_async_copy(back, back, back_send).wait()

    pltpu.make_async_copy(got, got, back_recv).wait()
    for tile in range(2):
        s = shift[2 * row + tile]
        side = slice(tile * BLOCK, (tile + 1) * BLOCK)
        for m in range(RH // 2):
            pair = []
            for e in (2 * m, 2 * m + 1):
                u = kept[tile, col, e] - s
                pair.append(got[jnp.where(u < 0, u + PANEL, u)][:, side])
            out_ref[tile, :, m * SPAN : (m + 1) * SPAN] = jnp.concatenate(pair, axis=1)


def body(density, density_rows, square_rows, panel_shift):
    bf16, f32, i32 = jnp.bfloat16, jnp.float32, jnp.int32
    dma = pltpu.SemaphoreType.DMA
    in_hbm = pl.BlockSpec(memory_space=pltpu.HBM)
    density, density_rows, square_rows, panel_shift = [
        pltpu.with_memory_space_constraint(v, pltpu.HBM)
        for v in (density, density_rows, square_rows, panel_shift)
    ]
    return pl.pallas_call(
        kernel,
        out_shape=jax.ShapeDtypeStruct((2, BLOCK, RH * BLOCK), bf16),
        in_specs=[in_hbm] * 4,
        out_specs=pl.BlockSpec(memory_space=pltpu.VMEM),
        scratch_shapes=[
            pltpu.VMEM((2, BLOCK, RH * BLOCK), bf16),
            pltpu.SMEM((2, N_COL, RH), i32),
            pltpu.VMEM((NPAN // 2, N_COL, RH), i32),
            pltpu.SMEM((2, N_COL, RH), i32),
            pltpu.SMEM((NPAN,), i32),
            pltpu.VMEM((PANEL, BLOCK, SPAN), bf16),
            pltpu.VMEM((2 * (RH + 1), BLOCK, SPAN), bf16),
            pltpu.VMEM((PANEL, BLOCK, SPAN), bf16),
            pltpu.VMEM((8, 4, 2, BLOCK, SPAN), bf16),
            pltpu.VMEM((FULL, FULL), bf16),
            pltpu.VMEM((HALF, FULL), f32),
            pltpu.VMEM((HALF, FULL), bf16),
            pltpu.VMEM((NPAN // 2, 8, FULL), f32),
            pltpu.VMEM((4, N_COL, BLOCK, SPAN), bf16),
            dma((5,)),
            dma,
            dma((8,)),
            dma,
            dma,
            dma,
            dma,
            pltpu.SemaphoreType.REGULAR,
        ],
        compiler_params=pltpu.CompilerParams(
            collective_id=0, has_side_effects=True, vmem_limit_bytes=40 * 2**20
        ),
    )(density, density_rows, square_rows, panel_shift).astype(f32)


def solution(mesh):
    placed = (P("row", None, "col"), P(), P(), P())
    return jax.shard_map(
        body, mesh=mesh, in_specs=placed, out_specs=P("row", None, "col"), check_vma=False
    )
```

```python
import itertools

import jax
import jax.numpy as jnp
from jax import lax
from jax.experimental import pallas as pl
from jax.experimental.pallas import tpu as pltpu
from jax.sharding import PartitionSpec as P

PANEL = 49
BLOCK = 64
SPAN = 2 * BLOCK
RH = 32
NPAN = 16
N_ROW = 8
N_COL = 16
HALF = NPAN * BLOCK // 2
FULL = NPAN * BLOCK
MESH = pl.DeviceIdType.MESH


def wrap(value, size):
    return jnp.where(value >= size, value - size, value)


def order():
    plain = list(itertools.product(range(4), repeat=3))
    return [plain[(i * 19 + 21) % 64] for i in range(64)]


def low_high(a, b):
    low = jnp.concatenate([a[:, :BLOCK], b[:, :BLOCK]], axis=1)
    high = jnp.concatenate([a[:, BLOCK:], b[:, BLOCK:]], axis=1)
    return low, high


def kernel(
    density, drows_hbm, srows_hbm, shift_hbm, out_ref,
    x_ref, drows, srows, kept, shift, got, blocks, send, recv, mat, acc, sq, mask, back,
    load_sem, send_sem, recv_sem, sib_send, sib_recv, back_send, back_recv, meet_sem,
):
    row = lax.axis_index("row")
    col = lax.axis_index("col")
    core = col % 2
    y = row % 4
    z_lo = row // 4
    x = col // 4
    z_hi = (col // 2) % 2
    z = 2 * z_hi + z_lo
    d = (x + y + z) % 4
    corner = (row + col // 2) == 0
    works = jnp.logical_or(d != 0, corner)
    mine = jnp.where(corner, PANEL - 1, (x * 4 + y) * 3 + d - 1)
    own = jnp.logical_and(works, core == z_lo)
    sibling = col + 1 - 2 * core

    loads = [
        pltpu.make_async_copy(density, x_ref, load_sem.at[0]),
        pltpu.make_async_copy(drows_hbm.at[pl.ds(2 * row, 2)], drows, load_sem.at[1]),
        pltpu.make_async_copy(shift_hbm, shift, load_sem.at[2]),
        pltpu.make_async_copy(srows_hbm.at[pl.ds(core * (NPAN // 2), NPAN // 2)], srows, load_sem.at[3]),
        pltpu.make_async_copy(srows_hbm.at[pl.ds(2 * row, 2)], kept, load_sem.at[4]),
    ]
    for load in loads:
        load.start()

    barrier = pltpu.get_barrier_semaphore()
    pl.semaphore_signal(barrier, inc=1, device_id=(row, sibling), device_id_type=MESH)
    told = x % 2
    lone = jnp.logical_and(own, told == core)

    @pl.when(works)
    def _():
        chip = col // 2
        for dy in range(4):
            to_row = 4 * core + wrap(y + dy, 4)
            for k in range(N_COL // 2):
                to_col = 2 * wrap(chip + k, N_COL // 2) + told

                def tell(to_row=to_row, to_col=to_col):
                    pl.semaphore_signal(barrier, inc=1, device_id=(to_row, to_col), device_id_type=MESH)

                if dy == k == 0:
                    pl.when(jnp.logical_not(lone))(tell)
                else:
                    tell()

    loads[0].wait()
    low_side = (lax.broadcasted_iota(jnp.int32, (1, SPAN), 1) < BLOCK).astype(jnp.bfloat16)
    sides = (low_side, 1 - low_side)
    for tile in range(2):
        for m in range(RH // 2):
            wide = x_ref[tile, :, m * SPAN : (m + 1) * SPAN]
            turned = jnp.concatenate([wide[:, BLOCK:], wide[:, :BLOCK]], axis=1)
            first, second = (wide, turned) if tile == 0 else (turned, wide)
            blocks[tile * (RH + 1) + 2 * m] = first * sides[tile]
            blocks[tile * (RH + 1) + 2 * m + 1] = second * sides[tile]
        blocks[tile * (RH + 1) + RH] = jnp.zeros((BLOCK, SPAN), jnp.bfloat16)

    loads[1].wait()
    loads[2].wait()
    loads[3].wait()
    loads[4].wait()

    pl.semaphore_wait(barrier, 1 + PANEL // 2 + (1 - core) - lone.astype(jnp.int32))
    pl.semaphore_signal(meet_sem, inc=1, device_id=(row, sibling), device_id_type=MESH)

    begin = []
    for tile in range(2):
        s = shift[2 * row + tile]
        e = jnp.int32(0)
        for i in range(RH):
            e = e + (drows[tile, col, i] < s).astype(jnp.int32)
        begin += [s, wrap(e, RH)]

    def fetch(u, carry):
        r0, e0, r1, e1 = carry
        hit0 = drows[0, col, e0] == r0
        hit1 = drows[1, col, e1] == r1
        send[u] = blocks[jnp.where(hit0, e0, RH)] + blocks[RH + 1 + jnp.where(hit1, e1, RH)]
        e0 = wrap(e0 + hit0.astype(jnp.int32), RH)
        e1 = wrap(e1 + hit1.astype(jnp.int32), RH)
        return wrap(r0 + 1, PANEL), e0, wrap(r1 + 1, PANEL), e1

    lax.fori_loop(0, PANEL, fetch, tuple(begin))

    pl.semaphore_wait(meet_sem, 1)

    xs = [wrap(x + k, 4) for k in range(4)]
    ys = [wrap(y + k, 4) for k in range(4)]

    def post(u, to_x, to_y, to_z, place, may_stay):
        slot = recv.at[place // 8, place % 8 // 2, core]
        arrived = recv_sem.at[place // 8]
        to_row = (to_z % 2) * 4 + to_y
        to_col = to_x * 4 + (to_z // 2) * 2 + z_lo

        def remote():
            pltpu.make_async_remote_copy(
                src_ref=send.at[u],
                dst_ref=slot,
                send_sem=send_sem,
                recv_sem=arrived,
                device_id=(to_row, to_col),
                device_id_type=MESH,
            ).start()

        def local():
            pltpu.make_async_copy(send.at[u], slot, arrived).start()

        if may_stay:
            stays = jnp.logical_and(to_row == row, to_col == col)
            pl.when(stays)(local)
            pl.when(jnp.logical_not(stays))(remote)
        else:
            remote()

    zs = [wrap(z + k, 4) for k in range(4)]
    ds = [wrap(d + k, 4) for k in range(4)]
    for place, (dx, dy, dz) in enumerate(order()):
        to_x, to_y, to_z, to_d = xs[dx], ys[dy], zs[dz], ds[(dx + dy + dz) % 4]
        u = jnp.where(to_d == 0, PANEL - 1, to_x * 12 + to_y * 3 + to_d - 1)

        @pl.when(jnp.logical_or(to_d != 0, (to_x + to_y + to_z) == 0))
        def _():
            post(u, to_x, to_y, to_z, place, dx == dy == dz == 0)

    @pl.when(works)
    def _():
        half = pl.multiple_of(core * HALF, HALF)
        there = pl.multiple_of((1 - core) * HALF, HALF)

        spread = jnp.where(
            lax.broadcasted_iota(jnp.int32, (NPAN, FULL), 1) // BLOCK
            == lax.broadcasted_iota(jnp.int32, (NPAN, FULL), 0),
            1.0,
            0.0,
        ).astype(jnp.bfloat16)
        for k in range(NPAN // 2):
            past = srows[k] - shift[core * (NPAN // 2) + k]
            hit = jnp.logical_or(past == mine, past == mine - PANEL)
            hit = jnp.where(hit, 1.0, 0.0).astype(jnp.bfloat16)
            count = lax.dot_general(
                jnp.ones((8, RH), jnp.bfloat16), hit, (((1,), (1,)), ((), ())),
                preferred_element_type=jnp.float32,
            ).astype(jnp.bfloat16)
            mask[k] = jnp.dot(count, spread, preferred_element_type=jnp.float32)

        straight = core == z_lo
        offsets = order()
        for k in range(8):
            pltpu.make_async_copy(recv.at[k], recv.at[k], recv_sem.at[k]).wait()
            for j in range(4):
                even, odd = sorted(offsets[8 * k + 2 * j : 8 * k + 2 * j + 2], key=lambda offset: offset[2] % 2)
                dx, dy, dz = (jnp.where(straight, one, other) for one, other in zip(even, odd))
                from_x, from_y, from_z = wrap(x + 4 - dx, 4), wrap(y + 4 - dy, 4), wrap(z + 4 - dz, 4)
                base = pl.multiple_of(core * HALF + from_y * SPAN, SPAN)
                at = pl.multiple_of((from_x * 2 + from_z // 2) * SPAN, SPAN)
                low, high = low_high(recv[k, j, 0], recv[k, j, 1])
                mat[pl.ds(base, BLOCK), pl.ds(at, SPAN)] = low
                mat[pl.ds(base + BLOCK, BLOCK), pl.ds(at, SPAN)] = high
                square = mat.at[pl.ds(base, SPAN), pl.ds(at, SPAN)]
                pltpu.make_async_remote_copy(
                    src_ref=square,
                    dst_ref=square,
                    send_sem=sib_send,
                    recv_sem=sib_recv,
                    device_id=(row, sibling),
                    device_id_type=MESH,
                ).start()

        acc[...] = jnp.dot(
            mat[pl.ds(half, HALF), pl.ds(half, HALF)],
            mat[pl.ds(half, HALF), :],
            preferred_element_type=jnp.float32,
        )

        came = mat.at[pl.ds(there, HALF)]
        pltpu.make_async_copy(came, came, sib_recv).wait()

        for n in range(FULL // 256):
            at = slice(n * 256, (n + 1) * 256)
            whole = acc[:, at] + jnp.dot(
                mat[pl.ds(half, HALF), pl.ds(there, HALF)],
                mat[pl.ds(there, HALF), at],
                preferred_element_type=jnp.float32,
            )
            for k in range(NPAN // 2):
                part = slice(k * BLOCK, (k + 1) * BLOCK)
                sq[part, at] = (whole[part] * mask[k, 0:1, at]).astype(jnp.bfloat16)

        def give(n, to_z, may_stay):
            for dy, dc in itertools.product((2, 1, 3, 0), range(2)):
                to_core = wrap(core + dc, 2)
                g = ys[dy]
                j = 4 * n + 2 * to_z + to_core
                to_row = 4 * core + g

                def remote(g=g, j=j, to_row=to_row):
                    pltpu.make_async_remote_copy(
                        src_ref=back.at[g, j],
                        dst_ref=got.at[mine],
                        send_sem=back_send,
                        recv_sem=back_recv,
                        device_id=(to_row, j),
                        device_id_type=MESH,
                    ).start()

                def local(g=g, j=j):
                    pltpu.make_async_copy(back.at[g, j], got.at[mine], back_recv).start()

                if may_stay and dy == 0:
                    stays = jnp.logical_and(to_row == row, j == col)
                    pl.when(stays)(local)
                    pl.when(jnp.logical_not(stays))(remote)
                else:
                    remote()

        for k, i in enumerate((2, 3, 1, 0)):
            n = xs[i]
            at = pl.multiple_of(n * 256, 256)
            cube = jnp.dot(sq[...], mat[:, pl.ds(at, 256)], preferred_element_type=jnp.float32)
            done = (3.0 * sq[:, pl.ds(at, 256)].astype(jnp.float32) - 2.0 * cube).astype(jnp.bfloat16)
            for g in range(4):
                for c in range(2):
                    top = done[g * SPAN : g * SPAN + BLOCK, c * SPAN : (c + 1) * SPAN]
                    under = done[g * SPAN + BLOCK : (g + 1) * SPAN, c * SPAN : (c + 1) * SPAN]
                    low, high = low_high(top, under)
                    back[g, 4 * n + 2 * c] = low
                    back[g, 4 * n + 2 * c + 1] = high
            give(n, 1 - z_hi, i == 0)
            give(n, z_hi, i == 0)

        went = mat.at[pl.ds(half, HALF)]
        pltpu.make_async_copy(went, went, sib_send).wait()

    @pl.when(own)
    def _():
        most = send.at[pl.ds(0, PANEL - 1)]
        pltpu.make_async_copy(most, most, send_sem).wait()

    @pl.when(jnp.logical_not(own))
    def _():
        pltpu.make_async_copy(send, send, send_sem).wait()

    @pl.when(own)
    def _():
        flat = back.reshape(4 * N_COL, BLOCK, SPAN).at[pl.ds(0, 4 * N_COL - 1)]
        pltpu.make_async_copy(flat, flat, back_send).wait()

    @pl.when(jnp.logical_and(works, jnp.logical_not(own)))
    def _():
        pltpu.make_async_copy(back, back, back_send).wait()

    pltpu.make_async_copy(got, got, back_recv).wait()
    for tile in range(2):
        s = shift[2 * row + tile]
        side = slice(tile * BLOCK, (tile + 1) * BLOCK)
        for m in range(RH // 2):
            pair = []
            for e in (2 * m, 2 * m + 1):
                u = kept[tile, col, e] - s
                pair.append(got[jnp.where(u < 0, u + PANEL, u)][:, side])
            out_ref[tile, :, m * SPAN : (m + 1) * SPAN] = jnp.concatenate(pair, axis=1).astype(jnp.float32)


def body(density, density_rows, square_rows, panel_shift):
    bf16, f32, i32 = jnp.bfloat16, jnp.float32, jnp.int32
    dma = pltpu.SemaphoreType.DMA
    in_hbm = pl.BlockSpec(memory_space=pltpu.HBM)
    density, density_rows, square_rows, panel_shift = [
        pltpu.with_memory_space_constraint(v, pltpu.HBM)
        for v in (density, density_rows, square_rows, panel_shift)
    ]
    return pl.pallas_call(
        kernel,
        out_shape=jax.ShapeDtypeStruct((2, BLOCK, RH * BLOCK), f32),
        in_specs=[in_hbm] * 4,
        out_specs=pl.BlockSpec(memory_space=pltpu.VMEM),
        scratch_shapes=[
            pltpu.VMEM((2, BLOCK, RH * BLOCK), bf16),
            pltpu.SMEM((2, N_COL, RH), i32),
            pltpu.VMEM((NPAN // 2, N_COL, RH), i32),
            pltpu.SMEM((2, N_COL, RH), i32),
            pltpu.SMEM((NPAN,), i32),
            pltpu.VMEM((PANEL, BLOCK, SPAN), bf16),
            pltpu.VMEM((2 * (RH + 1), BLOCK, SPAN), bf16),
            pltpu.VMEM((PANEL, BLOCK, SPAN), bf16),
            pltpu.VMEM((8, 4, 2, BLOCK, SPAN), bf16),
            pltpu.VMEM((FULL, FULL), bf16),
            pltpu.VMEM((HALF, FULL), f32),
            pltpu.VMEM((HALF, FULL), bf16),
            pltpu.VMEM((NPAN // 2, 8, FULL), f32),
            pltpu.VMEM((4, N_COL, BLOCK, SPAN), bf16),
            dma((5,)),
            dma,
            dma((8,)),
            dma,
            dma,
            dma,
            dma,
            pltpu.SemaphoreType.REGULAR,
        ],
        compiler_params=pltpu.CompilerParams(
            collective_id=0, has_side_effects=True, vmem_limit_bytes=40 * 2**20
        ),
    )(density, density_rows, square_rows, panel_shift)


def solution(mesh):
    placed = (P("row", None, "col"), P(), P(), P())
    return jax.shard_map(
        body, mesh=mesh, in_specs=placed, out_specs=P("row", None, "col"), check_vma=False
    )
```
